512 devices in a mesh: chain: 32 (over y, z_lo, core), block: 16 (over z_hi, x).
Axes of the slice: x: 4, y: 4, z: 16 (z_hi: 4, z_lo: 4; z = z_hi * 4 + z_lo), core: 2. Of those that a mesh axis runs over, the one named last changes fastest.
Arguments:
- state: bfloat16 [32, 16, 512, 512], P('chain', 'block'), may hold values from -400 to 400
- left_env: bfloat16 [32, 16, 2, 512, 512], P('chain', 'block'), may hold values from -1 to 5
- right_env: bfloat16 [32, 16, 2, 512, 512], P('chain', 'block'), may hold values from -1 to 5
- precond: float32 [32, 16, 512, 512], P('chain', 'block'), may hold values from 0.2 to 1
- ranks: int32 [32], P('chain'), may hold values from 1024 to 2048
Outputs:
- bond_out: bfloat16 [32, 16, 512, 512], P('chain', 'block')
The draws below stay inside these ranges and needn't reach their ends.
All inputs are finite; a program needn't handle non-finite values.
Results may differ from the reference program's by a relative error of at most 0.0063.
Values may be sent and summed in bfloat16 or wider, within the bound.
No kernel may reach another device: no remote copies, remote signals or barrier semaphores. Data moves between devices by JAX's collectives and lax.ppermute only.
A program may use at most 64 MiB of HBM per device.

```python
import math
import jax
import jax.numpy as jnp
from jax import lax

CHI = 2048
TERMS = 2
SEGS = 32
TILES = 16
GRID = 4
CB = 512


def draw_state(key, part):
    key_base, key_rows, key_cols = jax.random.split(key, 3)
    row_scale = jnp.exp(jax.random.uniform(key_rows, (SEGS, GRID, CB), jnp.float32, 0.0, math.log(10.0)))
    col_scale = jnp.exp(jax.random.uniform(key_cols, (SEGS, GRID, CB), jnp.float32, 0.0, math.log(10.0)))
    tile_index = jnp.arange(TILES, dtype=jnp.int32)
    rows_here = row_scale[:, tile_index // GRID][..., :, None]
    cols_here = col_scale[:, tile_index % GRID][..., None, :]
    base = jnp.clip(jax.random.normal(key_base, (SEGS, TILES, CB, CB), jnp.float32), -4.0, 4.0)
    return (base * rows_here * cols_here).astype(jnp.bfloat16)


def diagonal_part(key):
    key_seg, key_tile, key_rough = jax.random.split(key, 3)
    seg_level = jnp.exp(jax.random.uniform(key_seg, (SEGS, 1, 1), jnp.float32, math.log(0.5), math.log(1.5)))
    tile_level = jnp.exp(jax.random.uniform(key_tile, (SEGS, GRID, 1), jnp.float32, math.log(0.5), math.log(2.0)))
    rough = jnp.exp(jax.random.uniform(key_rough, (SEGS, GRID, CB), jnp.float32, math.log(0.7), math.log(1.4)))
    levels = seg_level * tile_level * rough
    tile_index = jnp.arange(TILES, dtype=jnp.int32)
    on_diag = (tile_index // GRID == tile_index % GRID).astype(jnp.float32)
    along = levels[:, tile_index % GRID] * on_diag[None, :, None]
    first_term = (jnp.arange(TERMS, dtype=jnp.int32) == 0).astype(jnp.float32)
    identity = jnp.eye(CB, dtype=jnp.float32)
    return first_term[None, None, :, None, None] * along[:, :, None, :, None] * identity[None, None, None, :, :]


def draw_left_env(key, part):
    own_key = jax.random.fold_in(key, 11)
    key_noise, key_diag = jax.random.split(own_key, 2)
    shape = (SEGS, TILES, TERMS, CB, CB)
    noise = jnp.clip(jax.random.normal(key_noise, shape, jnp.float32), -4.0, 4.0)
    noise = noise * (1.0 / math.sqrt(CHI))
    return (noise + diagonal_part(key_diag)).astype(jnp.bfloat16)


def draw_right_env(key, part):
    own_key = jax.random.fold_in(key, 23)
    key_noise, key_diag = jax.random.split(own_key, 2)
    shape = (SEGS, TILES, TERMS, CB, CB)
    noise = jnp.clip(jax.random.normal(key_noise, shape, jnp.float32), -4.0, 4.0)
    noise = noise * (1.0 / math.sqrt(CHI))
    return (noise + diagonal_part(key_diag)).astype(jnp.bfloat16)


def place_ends(drawn, rng, low, high):
    extent = drawn.shape
    place = [jax.random.randint(jax.random.fold_in(rng, axis), (), 0, extent[axis]) for axis in range(len(extent))]
    drawn = drawn.at[tuple(place)].set(low)
    longest = extent.index(max(extent))
    place[longest] = (place[longest] + 1) % extent[longest]
    return drawn.at[tuple(place)].set(high)


def block_levels(key, dims, cuts, smallest, top_value):
    def one(dim, blocks):
        steps = jax.random.uniform(jax.random.fold_in(jax.random.fold_in(key, 6), dim), (blocks,), jnp.float32, smallest / len(cuts), top_value / len(cuts))
        return jnp.repeat(jnp.exp(steps), dims[dim] // blocks).reshape((-1,) + (1,) * (len(dims) - dim - 1))

    loudness = one(*cuts[0])
    for cut in cuts[1:]:
        loudness = loudness * one(*cut)
    return loudness


def setup_inputs(seed: int = 0) -> dict:
    key_list = jax.random.split(jax.random.key(seed), 6)
    return {
        "state": draw_state(jax.random.fold_in(key_list[5], 71), 0),
        "left_env": draw_left_env(jax.random.fold_in(key_list[5], 71), 0),
        "right_env": draw_right_env(jax.random.fold_in(key_list[5], 71), 0),
        "precond": jnp.clip(jnp.exp(math.log(1.0) - 1.609438 * jax.random.uniform(key_list[3], (SEGS, TILES, CB, CB), jnp.float32) ** block_levels(key_list[3], (SEGS, TILES, CB, CB), ((0, 32), (1, 16)), -0.2, 0.2)), 0.2, 1.0),
        "ranks": place_ends(jax.random.randint(key_list[4], (SEGS,), CHI // 2, CHI + 1), jax.random.fold_in(key_list[4], 1), CHI // 2, CHI).astype(jnp.int32),
    }


def to_matrix(tiles):
    return tiles.reshape(GRID, GRID, CB, CB).transpose(0, 2, 1, 3).reshape(CHI, CHI)

def to_terms(tiles):
    return tiles.reshape(GRID, GRID, TERMS, CB, CB).transpose(2, 0, 3, 1, 4).reshape(TERMS, CHI, CHI)

def to_tiles(matrix):
    return matrix.reshape(GRID, CB, GRID, CB).transpose(0, 2, 1, 3).reshape(TILES, CB, CB)

def one_segment(pieces):
    state_tiles, left_tiles, right_tiles, scale_tiles, rank_limit = pieces
    state_matrix = to_matrix(state_tiles)
    lefts = to_terms(left_tiles)
    rights = to_terms(right_tiles)
    image = jnp.zeros((CHI, CHI), jnp.float32)
    for term in range(TERMS):
        middle = jnp.dot(state_matrix, rights[term], preferred_element_type=jnp.float32).astype(jnp.bfloat16)
        image = image + jnp.dot(lefts[term], middle, preferred_element_type=jnp.float32)
    state_f = state_matrix.astype(jnp.float32)
    energy = jnp.sum(state_f * image) / jnp.sum(state_f * state_f)
    index = jnp.arange(CHI, dtype=jnp.int32)
    keep_mask = ((index[:, None] < rank_limit) & (index[None, :] < rank_limit)).astype(jnp.float32)
    corrected = keep_mask * (state_f - (image - energy * state_f) * to_matrix(scale_tiles))
    normed = corrected / jnp.sqrt(jnp.mean(corrected * corrected) + 1e-06)
    return to_tiles(normed.astype(jnp.bfloat16))

def reference(state, left_env, right_env, precond, ranks):
    bonds = lax.map(one_segment, (state, left_env, right_env, precond, ranks))
    partners = bonds.reshape(SEGS // 2, 2, TILES, CB, CB)[:, ::-1].reshape(bonds.shape)
    paired = (0.75 * bonds.astype(jnp.float32) + 0.25 * partners.astype(jnp.float32)).astype(jnp.bfloat16)
    above = jnp.concatenate([paired[1:], paired[:1]], 0)
    below = jnp.concatenate([paired[-1:], paired[:-1]], 0)
    odd_seg = (jnp.arange(SEGS, dtype=jnp.int32) % 2 == 1)[:, None, None, None]
    partner = jnp.where(odd_seg, above, below)
    return (0.5 * (paired.astype(jnp.float32) + partner.astype(jnp.float32))).astype(jnp.bfloat16)
```

```python
import jax
import jax.numpy as jnp
from jax import lax
from jax.sharding import Mesh
from jax.sharding import PartitionSpec as P


BLOCK = ("block_0", "block_1")


def shift(value, axis, steps):
    count = lax.axis_size(axis)
    pairs = [(source, (source + steps) % count) for source in range(count)]
    return lax.ppermute(value, axis, pairs)


def even_partner(value):
    pairs = [(source, source ^ 1) for source in range(lax.axis_size("chain"))]
    return lax.ppermute(value, "chain", pairs)


def odd_partner(value):
    count = lax.axis_size("chain")
    pairs = [(source, (source + (1 if source % 2 else -1)) % count) for source in range(count)]
    return lax.ppermute(value, "chain", pairs)


def ring_pieces(value, axis):
    half = value.shape[-2] // 2
    behind = shift(value, axis, 1)
    ahead = shift(value, axis, -1)
    top = shift(behind[..., :half, :], axis, 1)
    bottom = shift(ahead[..., half:, :], axis, -1)
    return [value, behind, jnp.concatenate([top, bottom], axis=-2), ahead]


def mix_weighted(first_tile, second_tile, first_weight, second_weight):
    return (
        first_weight * first_tile.astype(jnp.float32)
        + second_weight * second_tile.astype(jnp.float32)
    ).astype(jnp.bfloat16)


def one_window(state, left_env, right_env, precond, ranks):
    side = lax.axis_size("block_0")
    row = lax.axis_index("block_0")
    col = lax.axis_index("block_1")
    state_tile = state[0, 0]
    left_tiles = left_env[0, 0]
    right_tiles = right_env[0, 0]
    scaling = precond[0, 0]
    terms = left_tiles.shape[0]
    width = state_tile.shape[0]
    order_full = side * width

    left_rows = lax.all_gather(left_tiles, "block_1", axis=0)
    state_pieces = ring_pieces(state_tile, "block_0")
    right_pieces = ring_pieces(right_tiles, "block_0")

    def block_of(gathered, distance):
        return lax.dynamic_index_in_dim(gathered, (row - distance) % side, 0, keepdims=False)

    partial = jnp.zeros((terms, width, width), jnp.float32)
    for distance in (0, 1, 3, 2):
        partial = partial + jnp.einsum(
            "kij,jl->kil",
            block_of(left_rows, distance),
            state_pieces[distance],
            preferred_element_type=jnp.float32,
        )
    turned_rows = lax.all_gather(partial.astype(jnp.bfloat16), "block_1", axis=0)
    image = jnp.zeros((width, width), jnp.float32)
    for distance in (0, 1, 3, 2):
        image = image + jnp.einsum(
            "kij,kjl->il",
            block_of(turned_rows, distance),
            right_pieces[distance],
            preferred_element_type=jnp.float32,
        )

    state_f = state_tile.astype(jnp.float32)
    row_index = row * width + jnp.arange(width, dtype=jnp.int32)
    col_index = col * width + jnp.arange(width, dtype=jnp.int32)
    rank_limit = ranks[0]
    keep_mask = ((row_index[:, None] < rank_limit) & (col_index[None, :] < rank_limit)).astype(
        jnp.float32
    )
    total_count = float(order_full * order_full)
    weighted = keep_mask * scaling
    state_sq = state_f * state_f
    cross_term = state_f * image
    moments = jnp.stack(
        [
            jnp.sum(state_sq),
            jnp.sum(cross_term),
            jnp.sum(keep_mask * state_sq),
            jnp.sum(weighted * state_sq),
            jnp.sum(weighted * scaling * state_sq),
            jnp.sum(weighted * cross_term),
            jnp.sum(weighted * scaling * cross_term),
            jnp.sum(weighted * scaling * image * image),
        ]
    )
    for axis in BLOCK:
        moments = lax.psum(moments, axis)
    norm_state, intersection, plain_sq, first_sq, second_sq, first_cross, second_cross, image_sq = (
        moments[index] for index in range(8)
    )
    energy = intersection / norm_state
    corrected = keep_mask * (state_f - (image - energy * state_f) * scaling)
    square_sum = (
        plain_sq
        + 2.0 * energy * first_sq
        + energy * energy * second_sq
        - 2.0 * first_cross
        - 2.0 * energy * second_cross
        + image_sq
    )
    bond = (corrected / jnp.sqrt(square_sum / total_count + 1e-06)).astype(jnp.bfloat16)
    own_pair = mix_weighted(bond, even_partner(bond), 0.75, 0.25)
    result = mix_weighted(own_pair, odd_partner(own_pair), 0.5, 0.5)
    return result[None, None]


def solution(mesh):
    split = Mesh(mesh.devices.reshape(mesh.shape["chain"], 4, 4), ("chain", "block_0", "block_1"))
    placed = (
        P("chain", BLOCK, None, None),
        P("chain", BLOCK, None, None, None),
        P("chain", BLOCK, None, None, None),
        P("chain", BLOCK, None, None),
        P("chain"),
    )
    return jax.shard_map(
        one_window,
        mesh=split,
        in_specs=placed,
        out_specs=P("chain", BLOCK, None, None),
        check_vma=False,
    )
```

```python
import jax
import jax.numpy as jnp
from jax import lax
from jax.sharding import Mesh
from jax.sharding import PartitionSpec as P


BLOCK = ("block_0", "block_1")
AXES = ("chain", "block_0", "block_1")
SIDE = 4


def permute(value, target):
    chain = lax.axis_size("chain")
    pairs = []
    for seg in range(chain):
        for row in range(SIDE):
            for col in range(SIDE):
                to = target(seg, row, col)
                if to is not None:
                    to_row, to_col = to
                    source = (seg * SIDE + row) * SIDE + col
                    pairs.append((source, (seg * SIDE + to_row) * SIDE + to_col))
    return lax.ppermute(value, AXES, pairs)


def is_active(seg, row):
    return row // 2 == seg % 2


def to_active(seg, row, col):
    return None if is_active(seg, row) else (row ^ 3, col)


def to_home(seg, row, col):
    return (row ^ 3, col) if is_active(seg, row) else None


def to_other(seg, row, col):
    return (row ^ 1, col) if is_active(seg, row) else None


def along_row(value):
    pieces = [value]
    for distance in (1, 2, 3):

        def target(seg, row, col, distance=distance):
            return (row, col ^ distance) if is_active(seg, row) else None

        pieces.append(permute(value, target))
    return jnp.stack(pieces)


def even_partner(value):
    pairs = [(source, source ^ 1) for source in range(lax.axis_size("chain"))]
    return lax.ppermute(value, "chain", pairs)


def odd_partner(value):
    count = lax.axis_size("chain")
    pairs = [(source, (source + (1 if source % 2 else -1)) % count) for source in range(count)]
    return lax.ppermute(value, "chain", pairs)


def after(value, *others):
    return lax.optimization_barrier((value, *others))[0]


def mix_weighted(first_tile, second_tile, first_weight, second_weight):
    return (
        first_weight * first_tile.astype(jnp.float32)
        + second_weight * second_tile.astype(jnp.float32)
    ).astype(jnp.bfloat16)


def one_window(state, left_env, right_env, precond, ranks):
    segment = lax.axis_index("chain")
    row = lax.axis_index("block_0")
    col = lax.axis_index("block_1")
    active = row // 2 == segment % 2
    state_tile = state[0, 0]
    left_tiles = left_env[0, 0]
    right_tiles = right_env[0, 0]
    scaling = precond[0, 0]
    width = state_tile.shape[0]
    half = width // 2
    order_full = SIDE * width

    state_far = permute(state_tile, to_active)
    left_far = permute(left_tiles, to_active)
    state_rows = [
        state_tile,
        permute(state_tile, to_other),
        permute(state_far, to_other),
        state_far,
    ]
    right_other = permute(right_tiles, to_other)
    right_parts = [right_tiles[..., :half], right_tiles[..., half:]]
    right_parts[0] = after(right_parts[0], left_far)
    right_far_0 = permute(right_parts[0], to_active)
    right_parts[1] = after(right_parts[1], right_far_0)
    right_far_1 = permute(right_parts[1], to_active)
    right_cross_0 = permute(right_far_0, to_other)
    right_cross_1 = permute(right_far_1, to_other)
    right_rows = (
        (right_tiles[..., :half], right_other[..., :half], right_cross_0, right_far_0),
        (right_tiles[..., half:], right_other[..., half:], right_cross_1, right_far_1),
    )

    place = col ^ row

    def block_of(stacked, j):
        return lax.dynamic_index_in_dim(stacked, place ^ j, 0, keepdims=False)

    def turn(left_stack):
        total = None
        for j in (0, 1, 3, 2):
            term = jnp.einsum(
                "kij,jl->kil",
                block_of(left_stack, j),
                state_rows[j],
                preferred_element_type=jnp.float32,
            )
            total = term if total is None else total + term
        return total.astype(jnp.bfloat16)

    def apply_right(turned_stack, rows):
        total = None
        for j in (0, 1, 3, 2):
            term = jnp.einsum(
                "kij,kjl->il",
                block_of(turned_stack, j),
                rows[j],
                preferred_element_type=jnp.float32,
            )
            total = term if total is None else total + term
        return total

    turned_own = along_row(turn(along_row(left_tiles)))
    turned_far = along_row(turn(along_row(left_far)))
    home_parts = []
    own_parts = []
    for part in (0, 1):
        far_image = apply_right(turned_far, right_rows[part]).astype(jnp.bfloat16)
        home_parts.append(permute(far_image, to_home))
        own_parts.append(apply_right(turned_own, right_rows[part]))
    image = jnp.where(
        active,
        jnp.concatenate(own_parts, axis=1),
        jnp.concatenate(home_parts, axis=1).astype(jnp.float32),
    )

    state_f = state_tile.astype(jnp.float32)
    row_index = row * width + jnp.arange(width, dtype=jnp.int32)
    col_index = col * width + jnp.arange(width, dtype=jnp.int32)
    rank_limit = ranks[0]
    keep_mask = ((row_index[:, None] < rank_limit) & (col_index[None, :] < rank_limit)).astype(
        jnp.float32
    )
    total_count = float(order_full * order_full)
    weighted = keep_mask * scaling
    state_sq = state_f * state_f
    cross_term = state_f * image
    terms = (
        state_sq,
        cross_term,
        keep_mask * state_sq,
        weighted * state_sq,
        weighted * scaling * state_sq,
        weighted * cross_term,
        weighted * scaling * cross_term,
        weighted * scaling * image * image,
    )
    moments = jnp.stack([jnp.sum(term, axis=0) for term in terms])
    for axis in BLOCK:
        moments = lax.psum(moments, axis)
    moments = jnp.sum(moments, axis=1)
    norm_state, intersection, plain_sq, first_sq, second_sq, first_cross, second_cross, image_sq = (
        moments[index] for index in range(8)
    )
    energy = intersection / norm_state
    corrected = keep_mask * (state_f - (image - energy * state_f) * scaling)
    square_sum = (
        plain_sq
        + 2.0 * energy * first_sq
        + energy * energy * second_sq
        - 2.0 * first_cross
        - 2.0 * energy * second_cross
        + image_sq
    )
    bond = (corrected / jnp.sqrt(square_sum / total_count + 1e-06)).astype(jnp.bfloat16)
    own_pair = mix_weighted(bond, even_partner(bond), 0.75, 0.25)
    result = mix_weighted(own_pair, odd_partner(own_pair), 0.5, 0.5)
    return result[None, None]


def solution(mesh):
    split = Mesh(mesh.devices.reshape(mesh.shape["chain"], SIDE, SIDE), AXES)
    placed = (
        P("chain", BLOCK, None, None),
        P("chain", BLOCK, None, None, None),
        P("chain", BLOCK, None, None, None),
        P("chain", BLOCK, None, None),
        P("chain"),
    )
    return jax.shard_map(
        one_window,
        mesh=split,
        in_specs=placed,
        out_specs=P("chain", BLOCK, None, None),
        check_vma=False,
    )
```
